256 devices in a mesh: group: 8 (over z_hi, core), shard: 32 (over z_lo, y, x).
Axes of the slice: x: 4, y: 4, z: 8 (z_hi: 4, z_lo: 2; z = z_hi * 2 + z_lo), core: 2. Of those that a mesh axis runs over, the one named last changes fastest.
Arguments:
- latents: bfloat16 [512, 32, 32, 320], P(('group', 'shard')), may hold values from -6 to 6
- cotangent: bfloat16 [512, 32, 32, 320], P(('group', 'shard')), may hold values from -6 to 6
- weights: float32 [8, 2880, 320], P('group', 'shard'), may hold values from -0.109375 to 0.109375
- momentum: float32 [8, 2880, 320], P('group', 'shard'), may hold values from -6 to 6
- step: int32 [1], replicated, may hold values from 0 to 63
Outputs:
- activations: float32 [512, 32, 32, 320], P(('group', 'shard'))
- data_grad: float32 [512, 32, 32, 320], P(('group', 'shard'))
- new_weights: float32 [8, 2880, 320], P('group', 'shard')
- new_momentum: float32 [8, 2880, 320], P('group', 'shard')
The draws below stay inside these ranges and needn't reach their ends.
Inputs may be any that keep to these rules, and one draw needn't show every extreme that they name: `step`: one value shared by all devices.
All inputs are finite; a program needn't handle non-finite values.
Results may differ from the reference program's by a relative error of at most 0.0029.
Values may be sent and summed in bfloat16 or wider, within the bound.
No kernel may reach another device: no remote copies, remote signals or barrier semaphores. Data moves between devices by JAX's collectives and lax.ppermute only.
A program may use at most 128 MiB of HBM per device.

```python
import jax
import jax.numpy as jnp
from jax import lax

C = 320
IMG_DEV = 2
HH = 32
WW = 32
IMAGES = 512
KROWS = 2880
N_GROUP = 8
N_SHARD = 32


def steps_of(stream_key, extent, pieces, least, largest):
    loudness, own = 1.0, jax.random.fold_in(stream_key, 6)
    for position, shards_of in pieces:
        steps = jnp.exp(jax.random.uniform(jax.random.fold_in(own, position), (shards_of,), jnp.float32, least / len(pieces), largest / len(pieces)))
        loudness = loudness * jnp.repeat(steps, extent[position] // shards_of).reshape([-1 if axis == position else 1 for axis in range(len(extent))])
    return loudness


def scatter_about(stream_key, extent, deviation, most, split=(), held_as=jnp.bfloat16):
    array = jax.random.normal(stream_key, extent, jnp.float32) * deviation
    if len(split) > 0:
        array = steps_of(stream_key, extent, split, -0.22, 0.18) * array
    return jnp.clip(array, min=-most, max=most).astype(held_as)


def setup_inputs(seed: int = 0) -> dict:
    seeds = jax.random.split(jax.random.key(seed), 6)
    latents = scatter_about(seeds[0], (IMAGES, HH, WW, C), 1.0, 6.0, ((0, 256),))
    cotangent = scatter_about(seeds[1], (IMAGES, HH, WW, C), 1.0, 6.0, ((0, 256),))
    weights = scatter_about(seeds[2], (N_GROUP, KROWS, C), (9 * C) ** -0.5, 0.109375, ((0, 8), (1, 32)), jnp.float32)
    momentum = scatter_about(seeds[3], (N_GROUP, KROWS, C), 1.0, 6.0, ((0, 8), (1, 32)), jnp.float32)
    step = jax.random.randint(seeds[4], (1,), 0, 64).astype(jnp.int32)
    return dict(latents=latents, cotangent=cotangent, weights=weights, momentum=momentum, step=step)


beta_rate = 0.9
peak_rate = 0.1
warm_steps = 64.0
tap_offsets = [(row_off, col_off) for row_off in (-1, 0, 1) for col_off in (-1, 0, 1)]


def shifted_view(padded, row_off, col_off):
    height = padded.shape[1] - 2
    width = padded.shape[2] - 2
    return padded[:, 1 + row_off:1 + row_off + height, 1 + col_off:1 + col_off + width, :]


def conv_step(latents, cotangent, kernel):
    channels = kernel.shape[1]
    image_shape = latents.shape
    cell_count = image_shape[0] * image_shape[1] * image_shape[2]
    pad_in = jnp.pad(latents, ((0, 0), (1, 1), (1, 1), (0, 0)))
    pad_co = jnp.pad(cotangent, ((0, 0), (1, 1), (1, 1), (0, 0)))
    flat_co = cotangent.reshape(cell_count, channels)
    forward = jnp.zeros((cell_count, channels), jnp.float32)
    backward = jnp.zeros((cell_count, channels), jnp.float32)
    tap_grads = []
    for tap_index, (row_off, col_off) in enumerate(tap_offsets):
        tap_kernel = kernel[tap_index * channels:(tap_index + 1) * channels]
        moved_in = shifted_view(pad_in, row_off, col_off).reshape(cell_count, channels)
        moved_co = shifted_view(pad_co, -row_off, -col_off).reshape(cell_count, channels)
        forward = forward + jnp.dot(moved_in, tap_kernel, preferred_element_type=jnp.float32)
        backward = backward + lax.dot_general(moved_co, tap_kernel, (((1,), (1,)), ((), ())), preferred_element_type=jnp.float32)
        tap_grads.append(lax.dot_general(moved_in, flat_co, (((0,), (0,)), ((), ())), preferred_element_type=jnp.float32))
    return (forward.reshape(image_shape),
            backward.reshape(image_shape),
            jnp.concatenate(tap_grads, 0))


def reference(latents, cotangent, weights, momentum, step):
    per_group = latents.shape[0] // N_GROUP
    grad_scale = float(N_SHARD * IMG_DEV * HH * WW) ** -0.5
    learn_rate = peak_rate * (step[0] + 1).astype(jnp.float32) / warm_steps
    acts_list = []
    back_list = []
    updated_list = []
    moment_list = []
    for group in range(N_GROUP):
        kernel = weights[group].astype(jnp.bfloat16)
        first = group * per_group

        def one_image(total, images):
            forward_img, backward_img, term = conv_step(images[0][None], images[1][None], kernel)
            return total + term, (forward_img[0], backward_img[0])

        total, outputs = lax.scan(one_image, jnp.zeros(kernel.shape, jnp.float32),
                                  (latents[first:first + per_group], cotangent[first:first + per_group]))
        acts_list.append(outputs[0])
        back_list.append(outputs[1])
        moment = beta_rate * momentum[group] + total * grad_scale
        moment_list.append(moment)
        updated_list.append(weights[group] - learn_rate * moment)
    updated = jnp.stack(updated_list, 0)
    moments = jnp.stack(moment_list, 0)
    bit_count = N_GROUP.bit_length() - 1
    distance = step[0] % bit_count
    partner = jnp.bitwise_xor(jnp.arange(N_GROUP, dtype=jnp.int32), jnp.left_shift(jnp.int32(1), distance.astype(jnp.int32)))
    new_weights = 0.5 * (updated + jnp.take(updated, partner, axis=0))
    new_momentum = 0.5 * (moments + jnp.take(moments, partner, axis=0))
    return (jnp.concatenate(acts_list, 0), jnp.concatenate(back_list, 0), new_weights, new_momentum)
```

```python
from functools import partial

import jax
import jax.numpy as jnp
from jax import lax
from jax.experimental import pallas as pl
from jax.experimental.pallas import tpu as pltpu
from jax.sharding import PartitionSpec as P


beta_rate = 0.9
peak_rate = 0.1
warm_steps = 64.0

BF = jnp.bfloat16
F32 = jnp.float32
CH = 320
LANES = 384
SIDE = 32
CELLS = SIDE * SIDE
PAD_CELLS = CELLS + 2 * SIDE
ROWS = 90
PARTS = 32
COLS = 1024
PACK = 240
KROWS = 9 * CH
VMEM_LIMIT = 60 * 1024 * 1024


def half_lanes(shape):
    return lax.broadcasted_iota(jnp.int32, shape, len(shape) - 1) < 64


def pack_rows(block):
    tail = block[:, 256:384]
    low, high = tail[0:48], pltpu.roll(tail[48:96], 64, 1)
    return block[:, 0:128], block[:, 128:256], jnp.where(half_lanes(low.shape), low, high)


def spread_kernel(w_ref, out_ref, stage):
    stage[...] = jnp.zeros_like(stage)
    stage[0:ROWS, 0:CH] = w_ref[...]
    first, second, third = pack_rows(stage[...])
    first, second, third = first.astype(BF), second.astype(BF), third.astype(BF)

    @pl.loop(0, PARTS)
    def _(j):
        out_ref[j, 0:96, :] = first
        out_ref[j, 96:192, :] = second
        out_ref[j, 192:240, :] = third


def build_columns(src_ref, image, stage, dst_ref, sign):
    stage[8 : 8 + CELLS, 0:CH] = src_ref[image].astype(F32)
    zero = jnp.zeros((SIDE, COLS), BF)
    dst_ref[image, 0:SIDE, :] = zero
    dst_ref[image, SIDE + CELLS : PAD_CELLS, :] = zero
    step = 128

    @pl.loop(0, CELLS // step)
    def _(k):
        start = pl.multiple_of(k * step, step)
        near = stage.at[pl.ds(start, step + 16), :]
        rest = []
        for b in (-1, 0, 1):
            off = sign * b
            value = near[8 + off : 8 + off + step, :]
            if off != 0:
                col = lax.broadcasted_iota(jnp.int32, value.shape, 0) % SIDE + off
                value = jnp.where((col >= 0) & (col < SIDE), value, 0.0)
            dst_ref[image, pl.ds(start + SIDE, step), 256 * (b + 1) : 256 * (b + 2)] = (
                value[:, 0:256].astype(BF)
            )
            rest.append(value[:, 256:384])
        low = half_lanes(rest[0].shape)
        first = jnp.where(low, rest[0], pltpu.roll(rest[1], 64, 1))
        second = jnp.where(low, rest[2], 0.0)
        dst_ref[image, pl.ds(start + SIDE, step), 768:896] = first.astype(BF)
        dst_ref[image, pl.ds(start + SIDE, step), 896:1024] = second.astype(BF)


def grad_kernel(x_ref, g_ref, out_ref, stage, cols, flipped, whole):
    for image in range(2):
        flipped[image] = jnp.transpose(x_ref[image])
        build_columns(g_ref, image, stage, cols, -1)
    for row in range(3):
        top = SIDE * (2 - row)
        for part in range(4):
            lanes = pl.ds(256 * part, 256)
            value = jnp.dot(
                flipped[0], cols[0, top : top + CELLS, lanes], preferred_element_type=F32
            ) + jnp.dot(flipped[1], cols[1, top : top + CELLS, lanes], preferred_element_type=F32)
            if part < 3:
                tap = 3 * row + part
                whole[CH * tap : CH * (tap + 1), 0:256] = value
            else:
                pieces = (value[:, 0:128], pltpu.roll(value[:, 0:128], 64, 1), value[:, 128:256])
                for b in range(3):
                    tap = 3 * row + b
                    whole[CH * tap : CH * (tap + 1), 256:384] = pieces[b]

    @pl.loop(0, PARTS // 4)
    def _(q):
        near = whole.at[pl.ds(pl.multiple_of(4 * ROWS * q, 8), 4 * ROWS + 8), :]
        for i in range(4):
            first, second, third = pack_rows(near[ROWS * i : ROWS * i + 96, :])
            out_ref[4 * q + i, 0:96, :] = first.astype(BF)
            out_ref[4 * q + i, 96:192, :] = second.astype(BF)
            out_ref[4 * q + i, 192:240, :] = third.astype(BF)


def unpack_kernel_rows(w_ref, whole):
    @pl.loop(0, PARTS // 4)
    def _(q):
        near = whole.at[pl.ds(pl.multiple_of(4 * ROWS * q, 8), 4 * ROWS + 8), :]
        for i in range(4):
            base, j = ROWS * i, 4 * q + i
            near[base : base + 96, 0:128] = w_ref[j, 0:96, :].astype(F32)
            near[base : base + 96, 128:256] = w_ref[j, 96:192, :].astype(F32)
            tail = w_ref[j, 192:240, :].astype(F32)
            near[base : base + 48, 256:384] = tail
            near[base + 48 : base + 96, 256:384] = pltpu.roll(tail, 64, 1)


def forward_kernel(x_ref, w_ref, out_ref, stage, cols, whole, taps):
    unpack_kernel_rows(w_ref, whole)
    for row in range(3):
        for b in range(3):
            base = CH * (3 * row + b)
            taps[row, 256 * b : 256 * (b + 1), :] = whole[base : base + 256, :].astype(BF)
            taps[row, 768 + 64 * b : 832 + 64 * b, :] = whole[base + 256 : base + 320, :].astype(BF)
        taps[row, 960:1024, :] = jnp.zeros((64, LANES), BF)
    for image in range(2):
        build_columns(x_ref, image, stage, cols, 1)
    block = 256
    for image in range(2):

        @pl.loop(0, CELLS // block)
        def _(m):
            start = pl.multiple_of(m * block, block)
            value = jnp.zeros((block, LANES), F32)
            for row in range(3):
                value += jnp.dot(
                    cols[image, pl.ds(start + SIDE * row, block), :],
                    taps[row],
                    preferred_element_type=F32,
                )
            out_ref[image, pl.ds(start, block), :] = value[:, 0:CH]


def backward_kernel(g_ref, w_ref, *refs, image):
    out_ref, stage, cols, whole, taps = refs[-5:]
    unpack_kernel_rows(w_ref, whole)
    for row in range(3):
        rest = []
        for b in range(3):
            base = CH * (3 * row + b)
            taps[row, :, 256 * b : 256 * (b + 1)] = whole[base : base + CH, 0:256].astype(BF)
            rest.append(whole[base : base + CH, 256:384])
        low = half_lanes(rest[0].shape)
        taps[row, :, 768:896] = jnp.where(low, rest[0], pltpu.roll(rest[1], 64, 1)).astype(BF)
        taps[row, :, 896:1024] = jnp.where(low, rest[2], 0.0).astype(BF)
    build_columns(g_ref, 0, stage, cols, -1)
    block = 256

    @pl.loop(0, CELLS // block)
    def _(m):
        start = pl.multiple_of(m * block, block)
        value = jnp.zeros((block, CH), F32)
        for row in range(3):
            value += lax.dot_general(
                cols[0, pl.ds(start + SIDE * (2 - row), block), :],
                taps[row],
                (((1,), (1,)), ((), ())),
                preferred_element_type=F32,
            )
        out_ref[0, pl.ds(start, block), :] = value


def sum_kernel(parts_ref, out_ref, low_ref):
    def body(j, total):
        return total + parts_ref[j].astype(F32)

    total = lax.fori_loop(1, PARTS, body, parts_ref[0].astype(F32))
    out_ref[...] = total
    low_ref[...] = total.astype(BF)


def update_kernel(step_ref, own_ref, other_ref, w_ref, m_ref, wp_ref, mp_ref, nw_ref, nm_ref, stage, *, scale):
    both = own_ref[...] + other_ref[...].astype(F32)
    stage[:, 0:128] = both[0:96]
    stage[:, 128:256] = both[96:192]
    stage[0:48, 256:384] = both[192:240]
    stage[48:96, 256:384] = pltpu.roll(both[192:240], 64, 1)
    rate = peak_rate * (step_ref[0] + 1).astype(F32) / warm_steps
    moment = (0.5 * beta_rate) * (m_ref[...] + mp_ref[...]) + (0.5 * scale) * stage[0:ROWS, 0:CH]
    nm_ref[...] = moment
    nw_ref[...] = 0.5 * (w_ref[...] + wp_ref[...]) - rate * moment


def call(kernel, outs, scratch, flops=0, moved=0, **kw):
    return pl.pallas_call(
        kernel,
        out_shape=outs,
        scratch_shapes=scratch,
        compiler_params=pltpu.CompilerParams(vmem_limit_bytes=VMEM_LIMIT),
        cost_estimate=pl.CostEstimate(flops=flops, bytes_accessed=moved, transcendentals=0),
        **kw,
    )


def branch(latents, cotangent, weights, momentum, step, level):
    mask = 2**level
    pairs = [(source, source ^ mask) for source in range(lax.axis_size("group"))]
    images = latents.shape[0]
    x = latents.reshape(images, CELLS, CH)
    g = cotangent.reshape(images, CELLS, CH)
    w, m = weights[0], momentum[0]
    packed = jax.ShapeDtypeStruct((PARTS, PACK, 128), BF)
    stage = pltpu.VMEM((CELLS + 16, LANES), F32)
    cols = pltpu.VMEM((2, PAD_CELLS, COLS), BF)
    whole = pltpu.VMEM((KROWS + 8, LANES), F32)
    conv_flops = 2 * images * CELLS * KROWS * CH

    spread = call(spread_kernel, packed, [pltpu.VMEM((96, LANES), F32)], moved=2000000)(w)
    gathered = lax.all_to_all(spread, "shard", 0, 0, tiled=True)
    wp = lax.ppermute(w, "group", pairs)
    mp = lax.ppermute(m, "group", pairs)
    terms = call(
        grad_kernel, packed,
        [stage, cols, pltpu.VMEM((2, CH, CELLS), BF), whole],
        flops=conv_flops, moved=5000000,
    )(x, g)
    terms, gathered = lax.optimization_barrier((terms, gathered))
    received = lax.all_to_all(terms, "shard", 0, 0, tiled=True)
    out = jax.ShapeDtypeStruct((images, CELLS, CH), F32)
    forward = call(
        forward_kernel, out,
        [stage, cols, whole, pltpu.VMEM((3, COLS, LANES), BF)],
        flops=conv_flops, moved=6000000,
    )(x, gathered)
    back = lambda into, image: call(
        partial(backward_kernel, image=image), out,
        [stage, pltpu.VMEM((1, PAD_CELLS, COLS), BF), whole, pltpu.VMEM((3, CH, COLS), BF)],
        flops=conv_flops // 2, moved=4000000,
        grid=(1,),
        in_specs=[
            pl.BlockSpec((1, CELLS, CH), lambda i: (image, 0, 0)),
            pl.BlockSpec((PARTS, PACK, 128), lambda i: (0, 0, 0)),
        ] + [pl.BlockSpec(memory_space=pl.ANY)] * len(into),
        out_specs=pl.BlockSpec((1, CELLS, CH), lambda i: (image, 0, 0)),
        input_output_aliases={2: 0} if into else {},
    )(g, gathered, *into)
    backward = [back([], 0)]
    own, own_low = call(
        sum_kernel,
        (jax.ShapeDtypeStruct((PACK, 128), F32), jax.ShapeDtypeStruct((PACK, 128), BF)),
        [], moved=2000000,
    )(received)
    other = lax.ppermute(own_low, "group", pairs)
    backward = back(backward, 1)
    cells_group = lax.axis_size("shard") * images * CELLS
    row_shape = jax.ShapeDtypeStruct((ROWS, CH), F32)
    vmem = pl.BlockSpec(memory_space=pltpu.VMEM)
    new_w, new_m = call(
        partial(update_kernel, scale=float(cells_group) ** (-0.5)),
        (row_shape, row_shape),
        [pltpu.VMEM((96, LANES), F32)],
        moved=1000000,
        in_specs=[pl.BlockSpec(memory_space=pltpu.SMEM)] + [vmem] * 6,
    )(step, own, other, w, m, wp, mp)
    return (
        forward.reshape(latents.shape),
        backward.reshape(latents.shape),
        new_w[None],
        new_m[None],
    )


def shards(latents, cotangent, weights, momentum, step):
    bit_count = lax.axis_size("group").bit_length() - 1
    branches = [partial(branch, level=level) for level in range(bit_count)]
    return lax.switch(step[0] % bit_count, branches, latents, cotangent, weights, momentum, step)


def solution(mesh):
    images = P(("group", "shard"), None, None, None)
    rows = P("group", "shard", None)
    return jax.shard_map(
        shards,
        mesh=mesh,
        in_specs=(images, images, rows, rows, P()),
        out_specs=(images, images, rows, rows),
        check_vma=False,
    )
```

```python
from functools import partial

import jax
import jax.numpy as jnp
from jax import lax
from jax.experimental import pallas as pl
from jax.experimental.pallas import tpu as pltpu
from jax.sharding import PartitionSpec as P


beta_rate = 0.9
peak_rate = 0.1
warm_steps = 64.0

BF = jnp.bfloat16
F32 = jnp.float32
CH = 320
LANES = 384
SIDE = 32
CELLS = SIDE * SIDE
PAD_CELLS = CELLS + 2 * SIDE
ROWS = 90
PARTS = 32
COLS = 1024
PACK = 240
KROWS = 9 * CH
VMEM_LIMIT = 26 * 1024 * 1024


def half_lanes(shape):
    return lax.broadcasted_iota(jnp.int32, shape, len(shape) - 1) < 64


def pack_rows(block):
    tail = block[:, 256:384]
    low, high = tail[0:48], pltpu.roll(tail[48:96], 64, 1)
    return block[:, 0:128], block[:, 128:256], jnp.where(half_lanes(low.shape), low, high)


def spread_kernel(w_ref, out_ref, stage):
    stage[...] = jnp.zeros_like(stage)
    stage[0:ROWS, 0:CH] = w_ref[:, 0, :]
    first, second, third = pack_rows(stage[...])
    first, second, third = first.astype(BF), second.astype(BF), third.astype(BF)

    @pl.loop(0, PARTS)
    def _(j):
        out_ref[j, 0:96, :] = first
        out_ref[j, 96:192, :] = second
        out_ref[j, 192:240, :] = third


def build_columns(src_ref, image, stage, dst_ref, sign):
    stage[8 : 8 + CELLS, 0:CH] = src_ref[image].astype(F32)
    zero = jnp.zeros((SIDE, COLS), BF)
    dst_ref[image, 0:SIDE, :] = zero
    dst_ref[image, SIDE + CELLS : PAD_CELLS, :] = zero
    step = 128

    @pl.loop(0, CELLS // step)
    def _(k):
        start = pl.multiple_of(k * step, step)
        near = stage.at[pl.ds(start, step + 16), :]
        rest = []
        for b in (-1, 0, 1):
            off = sign * b
            value = near[8 + off : 8 + off + step, :]
            if off != 0:
                col = lax.broadcasted_iota(jnp.int32, value.shape, 0) % SIDE + off
                value = jnp.where((col >= 0) & (col < SIDE), value, 0.0)
            dst_ref[image, pl.ds(start + SIDE, step), 256 * (b + 1) : 256 * (b + 2)] = (
                value[:, 0:256].astype(BF)
            )
            rest.append(value[:, 256:384])
        low = half_lanes(rest[0].shape)
        first = jnp.where(low, rest[0], pltpu.roll(rest[1], 64, 1))
        second = jnp.where(low, rest[2], 0.0)
        dst_ref[image, pl.ds(start + SIDE, step), 768:896] = first.astype(BF)
        dst_ref[image, pl.ds(start + SIDE, step), 896:1024] = second.astype(BF)


def grad_kernel(x_ref, g_ref, out_ref, stage, cols, flipped, whole):
    for image in range(2):
        flipped[image] = jnp.transpose(x_ref[image])
        build_columns(g_ref, image, stage, cols, -1)
    for row in range(3):
        top = SIDE * (2 - row)
        for part in range(4):
            lanes = pl.ds(256 * part, 256)
            value = jnp.dot(
                flipped[0], cols[0, top : top + CELLS, lanes], preferred_element_type=F32
            ) + jnp.dot(flipped[1], cols[1, top : top + CELLS, lanes], preferred_element_type=F32)
            if part < 3:
                tap = 3 * row + part
                whole[CH * tap : CH * (tap + 1), 0:256] = value
            else:
                pieces = (value[:, 0:128], pltpu.roll(value[:, 0:128], 64, 1), value[:, 128:256])
                for b in range(3):
                    tap = 3 * row + b
                    whole[CH * tap : CH * (tap + 1), 256:384] = pieces[b]

    @pl.loop(0, PARTS // 4)
    def _(q):
        near = whole.at[pl.ds(pl.multiple_of(4 * ROWS * q, 8), 4 * ROWS + 8), :]
        for i in range(4):
            first, second, third = pack_rows(near[ROWS * i : ROWS * i + 96, :])
            j = 4 * q + i
            out_ref[j, 0:96, :] = first.astype(BF)
            out_ref[j, 96:192, :] = second.astype(BF)
            out_ref[j, 192:240, :] = third.astype(BF)


def taps_kernel(w_ref, ahead_ref, back_ref, whole):
    @pl.loop(0, PARTS // 4)
    def _(q):
        near = whole.at[pl.ds(pl.multiple_of(4 * ROWS * q, 8), 4 * ROWS + 8), :]
        for i in range(4):
            base, j = ROWS * i, 4 * q + i
            near[base : base + 96, 0:128] = w_ref[j, 0:96, :].astype(F32)
            near[base : base + 96, 128:256] = w_ref[j, 96:192, :].astype(F32)
            tail = w_ref[j, 192:240, :].astype(F32)
            near[base : base + 48, 256:384] = tail
            near[base + 48 : base + 96, 256:384] = pltpu.roll(tail, 64, 1)

    for row in range(3):
        for b in range(3):
            base = CH * (3 * row + b)
            tap = whole[base : base + CH, :].astype(BF)
            turned = jnp.transpose(tap)
            ahead_ref[row, 256 * b : 256 * (b + 1), :] = tap[0:256]
            ahead_ref[row, 768 + 64 * b : 832 + 64 * b, :] = tap[256:320]
            back_ref[row, 256 * b : 256 * (b + 1), 0:CH] = turned[0:256]
            back_ref[row, 768 + 64 * b : 832 + 64 * b, 0:CH] = turned[256:320]
        ahead_ref[row, 960:1024, :] = jnp.zeros((64, LANES), BF)
        back_ref[row, 960:1024, :] = jnp.zeros((64, LANES), BF)


def conv_kernel(src_ref, taps_ref, *refs, sign):
    out_ref, stage, cols = refs[-3:]
    images = out_ref.shape[0]
    block = 256
    for image in range(images):
        build_columns(src_ref, image, stage, cols, sign)

        @pl.loop(0, CELLS // block)
        def _(m):
            start = pl.multiple_of(m * block, block)
            value = jnp.zeros((block, LANES), F32)
            for row in range(3):
                top = SIDE * (row if sign > 0 else 2 - row)
                value += jnp.dot(
                    cols[image, pl.ds(start + top, block), :],
                    taps_ref[row],
                    preferred_element_type=F32,
                )
            out_ref[image, pl.ds(start, block), :] = value[:, 0:CH]


def sum_kernel(parts_ref, own_ref, low_ref):
    def body(j, total):
        return total + parts_ref[j].astype(F32)

    own = lax.fori_loop(1, PARTS, body, parts_ref[0].astype(F32))
    own_ref[...] = own
    low_ref[...] = own.astype(BF)


def update_kernel(step_ref, own_ref, other_ref, w_ref, m_ref, wp_ref, mp_ref, nw_ref, nm_ref, stage, *, scale):
    both = own_ref[...] + other_ref[...].astype(F32)
    stage[:, 0:128] = both[0:96]
    stage[:, 128:256] = both[96:192]
    stage[0:48, 256:384] = both[192:240]
    stage[48:96, 256:384] = pltpu.roll(both[192:240], 64, 1)
    rate = peak_rate * (step_ref[0] + 1).astype(F32) / warm_steps
    moment = (0.5 * beta_rate) * (m_ref[:, 0, :] + mp_ref[:, 0, :]) + (0.5 * scale) * stage[0:ROWS, 0:CH]
    nm_ref[:, 0, :] = moment
    nw_ref[:, 0, :] = 0.5 * (w_ref[:, 0, :] + wp_ref[:, 0, :]) - rate * moment


def call(kernel, outs, scratch, flops=0, moved=0, **kw):
    return pl.pallas_call(
        kernel,
        out_shape=outs,
        scratch_shapes=scratch,
        compiler_params=pltpu.CompilerParams(vmem_limit_bytes=VMEM_LIMIT),
        cost_estimate=pl.CostEstimate(flops=flops, bytes_accessed=moved, transcendentals=0),
        **kw,
    )


def trade(bit, *values):
    mask = 2**bit
    pairs = [(source, source ^ mask) for source in range(lax.axis_size("group"))]
    return tuple(lax.ppermute(value, "group", pairs) for value in values)


def by_row(value):
    return jnp.transpose(value, (1, 0, 2))


def shards(latents, cotangent, weights, momentum, step):
    images = latents.shape[0]
    bit_count = lax.axis_size("group").bit_length() - 1
    level = step[0] % bit_count
    trades = [partial(trade, bit) for bit in range(bit_count)]
    x = latents.reshape(images, CELLS, CH)
    g = cotangent.reshape(images, CELLS, CH)
    w, m = by_row(weights), by_row(momentum)
    packed = jax.ShapeDtypeStruct((PARTS, PACK, 128), BF)
    stage = pltpu.VMEM((CELLS + 16, LANES), F32)
    cols = pltpu.VMEM((2, PAD_CELLS, COLS), BF)
    whole = pltpu.VMEM((KROWS + 8, LANES), F32)
    conv_flops = 2 * images * CELLS * KROWS * CH
    vmem = pl.BlockSpec(memory_space=pltpu.VMEM)

    spread = call(spread_kernel, packed, [pltpu.VMEM((96, LANES), F32)], moved=2000000)(w)
    gathered = lax.all_to_all(spread, "shard", 0, 0, tiled=True)
    terms = call(
        grad_kernel, packed,
        [stage, cols, pltpu.VMEM((2, CH, CELLS), BF), whole],
        flops=conv_flops, moved=5000000,
    )(x, g)
    terms, w_out, m_out = lax.optimization_barrier((terms, w, m))
    wp, mp = lax.switch(level, trades, w_out, m_out)
    terms, gathered, wp, mp = lax.optimization_barrier((terms, gathered, wp, mp))
    received = lax.all_to_all(terms, "shard", 0, 0, tiled=True)
    tap_shape = jax.ShapeDtypeStruct((3, COLS, LANES), BF)
    ahead, behind = call(
        taps_kernel, (tap_shape, tap_shape), [whole], flops=1000000, moved=6000000
    )(gathered)
    out = jax.ShapeDtypeStruct((images, CELLS, CH), F32)
    forward = call(
        partial(conv_kernel, sign=1), out, [stage, cols], flops=conv_flops, moved=6000000
    )(x, ahead)
    backward = call(
        partial(conv_kernel, sign=-1), out, [stage, cols], flops=conv_flops, moved=6000000
    )(g, behind)
    received, backward, forward = lax.optimization_barrier((received, backward, forward))
    own, own_low = call(
        sum_kernel, (jax.ShapeDtypeStruct((PACK, 128), F32), jax.ShapeDtypeStruct((PACK, 128), BF)),
        [], moved=2000000,
    )(received)
    (other,) = lax.switch(level, trades, own_low)
    cells_group = lax.axis_size("shard") * images * CELLS
    row_shape = jax.ShapeDtypeStruct((ROWS, 1, CH), F32)
    new_w, new_m = call(
        partial(update_kernel, scale=float(cells_group) ** (-0.5)),
        (row_shape, row_shape),
        [pltpu.VMEM((96, LANES), F32)],
        moved=1000000,
        in_specs=[pl.BlockSpec(memory_space=pltpu.SMEM)] + [vmem] * 6,
    )(step, own, other, w, m, wp, mp)
    return (
        forward.reshape(latents.shape),
        backward.reshape(latents.shape),
        by_row(new_w),
        by_row(new_m),
    )


def solution(mesh):
    images = P(("group", "shard"), None, None, None)
    rows = P("group", "shard", None)
    return jax.shard_map(
        shards,
        mesh=mesh,
        in_specs=(images, images, rows, rows, P()),
        out_specs=(images, images, rows, rows),
        check_vma=False,
    )
```

```python
from functools import partial

import jax
import jax.numpy as jnp
from jax import lax
from jax.experimental import pallas as pl
from jax.experimental.pallas import tpu as pltpu
from jax.sharding import PartitionSpec as P


beta_rate = 0.9
peak_rate = 0.1
warm_steps = 64.0

BF = jnp.bfloat16
F32 = jnp.float32
CH = 320
LANES = 384
SIDE = 32
CELLS = SIDE * SIDE
PAD_CELLS = CELLS + 2 * SIDE
ROWS = 90
PARTS = 32
COLS = 1024
PACK = 240
KROWS = 9 * CH
VMEM_LIMIT = 20 * 1024 * 1024


def half_lanes(shape):
    return lax.broadcasted_iota(jnp.int32, shape, len(shape) - 1) < 64


def pack_rows(block):
    tail = block[:, 256:384]
    low, high = tail[0:48], pltpu.roll(tail[48:96], 64, 1)
    return block[:, 0:128], block[:, 128:256], jnp.where(half_lanes(low.shape), low, high)


def spread_kernel(w_ref, out_ref, stage):
    stage[...] = jnp.zeros_like(stage)
    stage[0:ROWS, 0:CH] = w_ref[:, 0, :]
    first, second, third = pack_rows(stage[...])
    first, second, third = first.astype(BF), second.astype(BF), third.astype(BF)

    @pl.loop(0, PARTS)
    def _(j):
        out_ref[j, 0:96, :] = first
        out_ref[j, 96:192, :] = second
        out_ref[j, 192:240, :] = third


def build_columns(src_ref, image, stage, dst_ref, sign):
    stage[8 : 8 + CELLS, 0:CH] = src_ref[image].astype(F32)
    zero = jnp.zeros((SIDE, COLS), BF)
    dst_ref[image, 0:SIDE, :] = zero
    dst_ref[image, SIDE + CELLS : PAD_CELLS, :] = zero
    step = 128

    @pl.loop(0, CELLS // step)
    def _(k):
        start = pl.multiple_of(k * step, step)
        near = stage.at[pl.ds(start, step + 16), :]
        rest = []
        for b in (-1, 0, 1):
            off = sign * b
            value = near[8 + off : 8 + off + step, :]
            if off != 0:
                col = lax.broadcasted_iota(jnp.int32, value.shape, 0) % SIDE + off
                value = jnp.where((col >= 0) & (col < SIDE), value, 0.0)
            dst_ref[image, pl.ds(start + SIDE, step), 256 * (b + 1) : 256 * (b + 2)] = (
                value[:, 0:256].astype(BF)
            )
            rest.append(value[:, 256:384])
        low = half_lanes(rest[0].shape)
        first = jnp.where(low, rest[0], pltpu.roll(rest[1], 64, 1))
        second = jnp.where(low, rest[2], 0.0)
        dst_ref[image, pl.ds(start + SIDE, step), 768:896] = first.astype(BF)
        dst_ref[image, pl.ds(start + SIDE, step), 896:1024] = second.astype(BF)


def grad_kernel(x_ref, g_ref, out_ref, stage, cols, flipped, whole):
    for image in range(2):
        flipped[image] = jnp.transpose(x_ref[image])
        build_columns(g_ref, image, stage, cols, -1)
    for row in range(3):
        top = SIDE * (2 - row)
        for part in range(4):
            lanes = pl.ds(256 * part, 256)
            value = jnp.dot(
                flipped[0], cols[0, top : top + CELLS, lanes], preferred_element_type=F32
            ) + jnp.dot(flipped[1], cols[1, top : top + CELLS, lanes], preferred_element_type=F32)
            if part < 3:
                tap = 3 * row + part
                whole[CH * tap : CH * (tap + 1), 0:256] = value
            else:
                pieces = (value[:, 0:128], pltpu.roll(value[:, 0:128], 64, 1), value[:, 128:256])
                for b in range(3):
                    tap = 3 * row + b
                    whole[CH * tap : CH * (tap + 1), 256:384] = pieces[b]

    @pl.loop(0, PARTS // 4)
    def _(q):
        near = whole.at[pl.ds(pl.multiple_of(4 * ROWS * q, 8), 4 * ROWS + 8), :]
        for i in range(4):
            first, second, third = pack_rows(near[ROWS * i : ROWS * i + 96, :])
            j = 4 * q + i
            out_ref[j, 0:96, :] = first.astype(BF)
            out_ref[j, 96:192, :] = second.astype(BF)
            out_ref[j, 192:240, :] = third.astype(BF)


def taps_kernel(w_ref, ahead_ref, back_ref, whole):
    @pl.loop(0, PARTS // 4)
    def _(q):
        near = whole.at[pl.ds(pl.multiple_of(4 * ROWS * q, 8), 4 * ROWS + 8), :]
        for i in range(4):
            base, j = ROWS * i, 4 * q + i
            near[base : base + 96, 0:128] = w_ref[j, 0:96, :].astype(F32)
            near[base : base + 96, 128:256] = w_ref[j, 96:192, :].astype(F32)
            tail = w_ref[j, 192:240, :].astype(F32)
            near[base : base + 48, 256:384] = tail
            near[base + 48 : base + 96, 256:384] = pltpu.roll(tail, 64, 1)

    for row in range(3):
        for b in range(3):
            base = CH * (3 * row + b)
            tap = whole[base : base + CH, :].astype(BF)
            turned = jnp.transpose(tap)
            ahead_ref[row, 256 * b : 256 * (b + 1), :] = tap[0:256]
            ahead_ref[row, 768 + 64 * b : 832 + 64 * b, :] = tap[256:320]
            back_ref[row, 256 * b : 256 * (b + 1), 0:CH] = turned[0:256]
            back_ref[row, 768 + 64 * b : 832 + 64 * b, 0:CH] = turned[256:320]
        ahead_ref[row, 960:1024, :] = jnp.zeros((64, LANES), BF)
        back_ref[row, 960:1024, :] = jnp.zeros((64, LANES), BF)


def conv_kernel(src_ref, taps_ref, *refs, sign):
    out_ref, stage, cols = refs[-3:]
    images = out_ref.shape[0]
    block = 1024
    for image in range(images):
        build_columns(src_ref, image, stage, cols, sign)

        @pl.loop(0, CELLS // block)
        def _(m):
            start = pl.multiple_of(m * block, block)
            value = jnp.zeros((block, LANES), F32)
            for row in range(3):
                top = SIDE * (row if sign > 0 else 2 - row)
                value += jnp.dot(
                    cols[image, pl.ds(start + top, block), :],
                    taps_ref[row],
                    preferred_element_type=F32,
                )
            out_ref[image, pl.ds(start, block), :] = value[:, 0:CH]


def sum_kernel(parts_ref, own_ref, low_ref):
    def body(j, total):
        return total + parts_ref[j].astype(F32)

    own = lax.fori_loop(1, PARTS, body, parts_ref[0].astype(F32))
    own_ref[...] = own
    low_ref[...] = own.astype(BF)


def update_kernel(step_ref, own_ref, other_ref, w_ref, m_ref, wp_ref, mp_ref, nw_ref, nm_ref, stage, *, scale):
    both = own_ref[...] + other_ref[...].astype(F32)
    stage[:, 0:128] = both[0:96]
    stage[:, 128:256] = both[96:192]
    stage[0:48, 256:384] = both[192:240]
    stage[48:96, 256:384] = pltpu.roll(both[192:240], 64, 1)
    rate = peak_rate * (step_ref[0] + 1).astype(F32) / warm_steps
    moment = (0.5 * beta_rate) * (m_ref[:, 0, :] + mp_ref[:, 0, :]) + (0.5 * scale) * stage[0:ROWS, 0:CH]
    nm_ref[:, 0, :] = moment
    nw_ref[:, 0, :] = 0.5 * (w_ref[:, 0, :] + wp_ref[:, 0, :]) - rate * moment


def call(kernel, outs, scratch, flops=0, moved=0, **kw):
    return pl.pallas_call(
        kernel,
        out_shape=outs,
        scratch_shapes=scratch,
        compiler_params=pltpu.CompilerParams(vmem_limit_bytes=VMEM_LIMIT),
        cost_estimate=pl.CostEstimate(flops=flops, bytes_accessed=moved, transcendentals=0),
        **kw,
    )


def trade(bit, *values):
    mask = 2**bit
    pairs = [(source, source ^ mask) for source in range(lax.axis_size("group"))]
    return tuple(lax.ppermute(value, "group", pairs) for value in values)


def by_row(value):
    return jnp.transpose(value, (1, 0, 2))


def shards(latents, cotangent, weights, momentum, step):
    images = latents.shape[0]
    bit_count = lax.axis_size("group").bit_length() - 1
    level = step[0] % bit_count
    trades = [partial(trade, bit) for bit in range(bit_count)]
    x = latents.reshape(images, CELLS, CH)
    g = cotangent.reshape(images, CELLS, CH)
    w, m = by_row(weights), by_row(momentum)
    packed = jax.ShapeDtypeStruct((PARTS, PACK, 128), BF)
    stage = pltpu.VMEM((CELLS + 16, LANES), F32)
    cols = pltpu.VMEM((2, PAD_CELLS, COLS), BF)
    whole = pltpu.VMEM((KROWS + 8, LANES), F32)
    conv_flops = 2 * images * CELLS * KROWS * CH
    vmem = pl.BlockSpec(memory_space=pltpu.VMEM)

    spread = call(spread_kernel, packed, [pltpu.VMEM((96, LANES), F32)], moved=2000000)(w)
    gathered = lax.all_to_all(spread, "shard", 0, 0, tiled=True)

    def begin(bit, w, m, x, g):
        wp, mp = trade(bit, w, m)
        terms = call(
            grad_kernel, packed,
            [stage, cols, pltpu.VMEM((2, CH, CELLS), BF), whole],
            flops=conv_flops, moved=5000000,
        )(x, g)
        return wp, mp, terms

    begins = [partial(begin, bit) for bit in range(bit_count)]
    wp, mp, terms = lax.switch(level, begins, w, m, x, g)
    terms, gathered, wp, mp = lax.optimization_barrier((terms, gathered, wp, mp))
    received = lax.all_to_all(terms, "shard", 0, 0, tiled=True)
    tap_shape = jax.ShapeDtypeStruct((3, COLS, LANES), BF)
    ahead, behind = call(
        taps_kernel, (tap_shape, tap_shape), [whole], flops=1000000, moved=6000000
    )(gathered)
    out = jax.ShapeDtypeStruct((images, CELLS, CH), F32)
    forward = call(
        partial(conv_kernel, sign=1), out, [stage, cols], flops=conv_flops, moved=6000000
    )(x, ahead)
    backward = call(
        partial(conv_kernel, sign=-1), out, [stage, cols], flops=conv_flops, moved=6000000
    )(g, behind)
    own, own_low = call(
        sum_kernel, (jax.ShapeDtypeStruct((PACK, 128), F32), jax.ShapeDtypeStruct((PACK, 128), BF)),
        [], moved=2000000,
    )(received)
    (other,) = lax.switch(level, trades, own_low)
    cells_group = lax.axis_size("shard") * images * CELLS
    row_shape = jax.ShapeDtypeStruct((ROWS, 1, CH), F32)
    new_w, new_m = call(
        partial(update_kernel, scale=float(cells_group) ** (-0.5)),
        (row_shape, row_shape),
        [pltpu.VMEM((96, LANES), F32)],
        moved=1000000,
        in_specs=[pl.BlockSpec(memory_space=pltpu.SMEM)] + [vmem] * 6,
    )(step, own, other, w, m, wp, mp)
    return (
        forward.reshape(latents.shape),
        backward.reshape(latents.shape),
        by_row(new_w),
        by_row(new_m),
    )


def solution(mesh):
    images = P(("group", "shard"), None, None, None)
    rows = P("group", "shard", None)
    return jax.shard_map(
        shards,
        mesh=mesh,
        in_specs=(images, images, rows, rows, P()),
        out_specs=(images, images, rows, rows),
        check_vma=False,
    )
```

```python
from functools import partial

import jax
import jax.numpy as jnp
from jax import lax
from jax.experimental import pallas as pl
from jax.experimental.pallas import tpu as pltpu
from jax.sharding import PartitionSpec as P


beta_rate = 0.9
peak_rate = 0.1
warm_steps = 64.0

BF = jnp.bfloat16
F32 = jnp.float32
CH = 320
LANES = 384
SIDE = 32
CELLS = SIDE * SIDE
PAD_CELLS = CELLS + 2 * SIDE
ROWS = 90
PARTS = 32
COLS = 1024
PACK = 240
KROWS = 9 * CH
VMEM_LIMIT = 20 * 1024 * 1024


def half_lanes(shape):
    return lax.broadcasted_iota(jnp.int32, shape, len(shape) - 1) < 64


def pack_rows(block):
    tail = block[:, 256:384]
    low, high = tail[0:48], pltpu.roll(tail[48:96], 64, 1)
    return block[:, 0:128], block[:, 128:256], jnp.where(half_lanes(low.shape), low, high)


def pack_into(rows_ref, stage, out_ref):
    stage[0:ROWS, 0:CH] = rows_ref[:, 0, :]
    first, second, third = pack_rows(stage[...])
    out_ref[0:96, :] = first.astype(BF)
    out_ref[96:192, :] = second.astype(BF)
    out_ref[192:240, :] = third.astype(BF)


def unpack_into(stage, value):
    stage[:, 0:128] = value[0:96]
    stage[:, 128:256] = value[96:192]
    stage[0:48, 256:384] = value[192:240]
    stage[48:96, 256:384] = pltpu.roll(value[192:240], 64, 1)


def pack_kernel(rows_ref, out_ref, stage):
    stage[...] = jnp.zeros_like(stage)
    pack_into(rows_ref, stage, out_ref)


def spread_kernel(w_ref, out_ref, wp_ref, stage):
    pack_kernel(w_ref, wp_ref, stage)
    piece = wp_ref[...]

    @pl.loop(0, PARTS)
    def _(j):
        out_ref[j] = piece


def build_columns(src_ref, image, stage, dst_ref, sign):
    stage[8 : 8 + CELLS, 0:CH] = src_ref[image].astype(F32)
    zero = jnp.zeros((SIDE, COLS), BF)
    dst_ref[image, 0:SIDE, :] = zero
    dst_ref[image, SIDE + CELLS : PAD_CELLS, :] = zero
    step = 128

    @pl.loop(0, CELLS // step)
    def _(k):
        start = pl.multiple_of(k * step, step)
        near = stage.at[pl.ds(start, step + 16), :]
        rest = []
        for b in (-1, 0, 1):
            off = sign * b
            value = near[8 + off : 8 + off + step, :]
            if off != 0:
                col = lax.broadcasted_iota(jnp.int32, value.shape, 0) % SIDE + off
                value = jnp.where((col >= 0) & (col < SIDE), value, 0.0)
            dst_ref[image, pl.ds(start + SIDE, step), 256 * (b + 1) : 256 * (b + 2)] = (
                value[:, 0:256].astype(BF)
            )
            rest.append(value[:, 256:384])
        low = half_lanes(rest[0].shape)
        first = jnp.where(low, rest[0], pltpu.roll(rest[1], 64, 1))
        second = jnp.where(low, rest[2], 0.0)
        dst_ref[image, pl.ds(start + SIDE, step), 768:896] = first.astype(BF)
        dst_ref[image, pl.ds(start + SIDE, step), 896:1024] = second.astype(BF)


def grad_kernel(x_ref, g_ref, out_ref, stage, cols, flipped, whole):
    for image in range(2):
        flipped[image] = jnp.transpose(x_ref[image])
        build_columns(g_ref, image, stage, cols, -1)
    for row in range(3):
        top = SIDE * (2 - row)
        for part in range(4):
            lanes = pl.ds(256 * part, 256)
            value = jnp.dot(
                flipped[0], cols[0, top : top + CELLS, lanes], preferred_element_type=F32
            ) + jnp.dot(flipped[1], cols[1, top : top + CELLS, lanes], preferred_element_type=F32)
            if part < 3:
                tap = 3 * row + part
                whole[CH * tap : CH * (tap + 1), 0:256] = value
            else:
                pieces = (value[:, 0:128], pltpu.roll(value[:, 0:128], 64, 1), value[:, 128:256])
                for b in range(3):
                    tap = 3 * row + b
                    whole[CH * tap : CH * (tap + 1), 256:384] = pieces[b]

    @pl.loop(0, PARTS // 4)
    def _(q):
        near = whole.at[pl.ds(pl.multiple_of(4 * ROWS * q, 8), 4 * ROWS + 8), :]
        for i in range(4):
            first, second, third = pack_rows(near[ROWS * i : ROWS * i + 96, :])
            j = 4 * q + i
            out_ref[j, 0:96, :] = first.astype(BF)
            out_ref[j, 96:192, :] = second.astype(BF)
            out_ref[j, 192:240, :] = third.astype(BF)


def taps_kernel(w_ref, ahead_ref, back_ref, whole):
    @pl.loop(0, PARTS // 4)
    def _(q):
        near = whole.at[pl.ds(pl.multiple_of(4 * ROWS * q, 8), 4 * ROWS + 8), :]
        for i in range(4):
            base, j = ROWS * i, 4 * q + i
            near[base : base + 96, 0:128] = w_ref[j, 0:96, :].astype(F32)
            near[base : base + 96, 128:256] = w_ref[j, 96:192, :].astype(F32)
            tail = w_ref[j, 192:240, :].astype(F32)
            near[base : base + 48, 256:384] = tail
            near[base + 48 : base + 96, 256:384] = pltpu.roll(tail, 64, 1)

    for row in range(3):
        for b in range(3):
            base = CH * (3 * row + b)
            tap = whole[base : base + CH, :].astype(BF)
            turned = jnp.transpose(tap)
            ahead_ref[row, 256 * b : 256 * (b + 1), :] = tap[0:256]
            ahead_ref[row, 768 + 64 * b : 832 + 64 * b, :] = tap[256:320]
            back_ref[row, 256 * b : 256 * (b + 1), 0:CH] = turned[0:256]
            back_ref[row, 768 + 64 * b : 832 + 64 * b, 0:CH] = turned[256:320]
        ahead_ref[row, 960:1024, :] = jnp.zeros((64, LANES), BF)
        back_ref[row, 960:1024, :] = jnp.zeros((64, LANES), BF)


def conv_kernel(src_ref, taps_ref, *refs, sign):
    out_ref, stage, cols = refs[-3:]
    images = out_ref.shape[0]
    block = 1024
    for image in range(images):
        build_columns(src_ref, image, stage, cols, sign)

        @pl.loop(0, CELLS // block)
        def _(m):
            start = pl.multiple_of(m * block, block)
            value = jnp.zeros((block, LANES), F32)
            for row in range(3):
                top = SIDE * (row if sign > 0 else 2 - row)
                value += jnp.dot(
                    cols[image, pl.ds(start + top, block), :],
                    taps_ref[row],
                    preferred_element_type=F32,
                )
            out_ref[image, pl.ds(start, block), :] = value[:, 0:CH]


def sum_kernel(parts_ref, own_ref, low_ref):
    def body(j, total):
        return total + parts_ref[j].astype(F32)

    own = lax.fori_loop(1, PARTS, body, parts_ref[0].astype(F32))
    own_ref[...] = own
    low_ref[...] = own.astype(BF)


def update_kernel(step_ref, own_ref, other_ref, w_ref, m_ref, wp_ref, mp_ref, nw_ref, nm_ref, stage, *, scale):
    both = own_ref[...] + other_ref[...].astype(F32)
    unpack_into(stage, (0.5 * beta_rate) * mp_ref[...].astype(F32) + (0.5 * scale) * both)
    rate = peak_rate * (step_ref[0] + 1).astype(F32) / warm_steps
    moment = (0.5 * beta_rate) * m_ref[:, 0, :] + stage[0:ROWS, 0:CH]
    nm_ref[:, 0, :] = moment
    unpack_into(stage, 0.5 * wp_ref[...].astype(F32))
    nw_ref[:, 0, :] = 0.5 * w_ref[:, 0, :] + stage[0:ROWS, 0:CH] - rate * moment


def call(kernel, outs, scratch, flops=0, moved=0, **kw):
    return pl.pallas_call(
        kernel,
        out_shape=outs,
        scratch_shapes=scratch,
        compiler_params=pltpu.CompilerParams(vmem_limit_bytes=VMEM_LIMIT),
        cost_estimate=pl.CostEstimate(flops=flops, bytes_accessed=moved, transcendentals=0),
        **kw,
    )


def trade(bit, *values):
    mask = 2**bit
    pairs = [(source, source ^ mask) for source in range(lax.axis_size("group"))]
    return tuple(lax.ppermute(value, "group", pairs) for value in values)


def by_row(value):
    return jnp.transpose(value, (1, 0, 2))


def shards(latents, cotangent, weights, momentum, step):
    images = latents.shape[0]
    bit_count = lax.axis_size("group").bit_length() - 1
    level = step[0] % bit_count
    trades = [partial(trade, bit) for bit in range(bit_count)]
    x = latents.reshape(images, CELLS, CH)
    g = cotangent.reshape(images, CELLS, CH)
    w, m = by_row(weights), by_row(momentum)
    packed = jax.ShapeDtypeStruct((PARTS, PACK, 128), BF)
    stage = pltpu.VMEM((CELLS + 16, LANES), F32)
    cols = pltpu.VMEM((2, PAD_CELLS, COLS), BF)
    whole = pltpu.VMEM((KROWS + 8, LANES), F32)
    conv_flops = 2 * images * CELLS * KROWS * CH
    vmem = pl.BlockSpec(memory_space=pltpu.VMEM)

    piece = jax.ShapeDtypeStruct((PACK, 128), BF)
    pack_stage = pltpu.VMEM((96, LANES), F32)
    spread, w_low = call(spread_kernel, (packed, piece), [pack_stage], moved=2000000)(w)
    m_late, w_low = lax.optimization_barrier((m, w_low))
    m_low = call(pack_kernel, piece, [pack_stage], moved=200000)(m_late)
    gathered = lax.all_to_all(spread, "shard", 0, 0, tiled=True)

    def begin(bit, w, m, x, g):
        wp, mp = trade(bit, w, m)
        terms = call(
            grad_kernel, packed,
            [stage, cols, pltpu.VMEM((2, CH, CELLS), BF), whole],
            flops=conv_flops, moved=5000000,
        )(x, g)
        return wp, mp, terms

    begins = [partial(begin, bit) for bit in range(bit_count)]
    wp, mp, terms = lax.switch(level, begins, w_low, m_low, x, g)
    terms, gathered, wp, mp = lax.optimization_barrier((terms, gathered, wp, mp))
    received = lax.all_to_all(terms, "shard", 0, 0, tiled=True)
    tap_shape = jax.ShapeDtypeStruct((3, COLS, LANES), BF)
    ahead, behind = call(
        taps_kernel, (tap_shape, tap_shape), [whole], flops=1000000, moved=6000000
    )(gathered)
    out = jax.ShapeDtypeStruct((images, CELLS, CH), F32)
    forward = call(
        partial(conv_kernel, sign=1), out, [stage, cols], flops=conv_flops, moved=6000000
    )(x, ahead)
    backward = call(
        partial(conv_kernel, sign=-1), out, [stage, cols], flops=conv_flops, moved=6000000
    )(g, behind)
    own, own_low = call(
        sum_kernel, (jax.ShapeDtypeStruct((PACK, 128), F32), jax.ShapeDtypeStruct((PACK, 128), BF)),
        [], moved=2000000,
    )(received)
    (other,) = lax.switch(level, trades, own_low)
    cells_group = lax.axis_size("shard") * images * CELLS
    row_shape = jax.ShapeDtypeStruct((ROWS, 1, CH), F32)
    new_w, new_m = call(
        partial(update_kernel, scale=float(cells_group) ** (-0.5)),
        (row_shape, row_shape),
        [pltpu.VMEM((96, LANES), F32)],
        moved=1000000,
        in_specs=[pl.BlockSpec(memory_space=pltpu.SMEM)] + [vmem] * 6,
    )(step, own, other, w, m, wp, mp)
    return (
        forward.reshape(latents.shape),
        backward.reshape(latents.shape),
        by_row(new_w),
        by_row(new_m),
    )


def solution(mesh):
    images = P(("group", "shard"), None, None, None)
    rows = P("group", "shard", None)
    return jax.shard_map(
        shards,
        mesh=mesh,
        in_specs=(images, images, rows, rows, P()),
        out_specs=(images, images, rows, rows),
        check_vma=False,
    )
```

```python
from functools import partial

import jax
import jax.numpy as jnp
from jax import lax
from jax.experimental import pallas as pl
from jax.experimental.pallas import tpu as pltpu
from jax.sharding import PartitionSpec as P


beta_rate = 0.9
peak_rate = 0.1
warm_steps = 64.0

BF = jnp.bfloat16
F32 = jnp.float32
CH = 320
LANES = 384
SIDE = 32
CELLS = SIDE * SIDE
PAD_CELLS = CELLS + 2 * SIDE
ROWS = 90
PARTS = 32
COLS = 1024
PACK = 240
KROWS = 9 * CH
VMEM_LIMIT = 20 * 1024 * 1024


def half_lanes(shape):
    return lax.broadcasted_iota(jnp.int32, shape, len(shape) - 1) < 64


def pack_rows(block):
    tail = block[:, 256:384]
    low, high = tail[0:48], pltpu.roll(tail[48:96], 64, 1)
    return block[:, 0:128], block[:, 128:256], jnp.where(half_lanes(low.shape), low, high)


def pack_into(rows_ref, stage, out_ref):
    stage[0:ROWS, 0:CH] = rows_ref[:, 0, :]
    first, second, third = pack_rows(stage[...])
    out_ref[0:96, :] = first.astype(BF)
    out_ref[96:192, :] = second.astype(BF)
    out_ref[192:240, :] = third.astype(BF)


def unpack_into(stage, value):
    stage[:, 0:128] = value[0:96]
    stage[:, 128:256] = value[96:192]
    stage[0:48, 256:384] = value[192:240]
    stage[48:96, 256:384] = pltpu.roll(value[192:240], 64, 1)


def pack_kernel(rows_ref, out_ref, stage):
    stage[...] = jnp.zeros_like(stage)
    pack_into(rows_ref, stage, out_ref)


def pair_kernel(w_low_ref, m_ref, out_ref, stage):
    out_ref[0] = w_low_ref[...]
    pack_kernel(m_ref, out_ref.at[1], stage)


def spread_kernel(w_ref, out_ref, wp_ref, stage):
    pack_kernel(w_ref, wp_ref, stage)
    piece = wp_ref[...]

    @pl.loop(0, PARTS)
    def _(j):
        out_ref[j] = piece


def build_columns(src_ref, image, stage, dst_ref, sign):
    stage[8 : 8 + CELLS, 0:CH] = src_ref[image].astype(F32)
    zero = jnp.zeros((SIDE, COLS), BF)
    dst_ref[image, 0:SIDE, :] = zero
    dst_ref[image, SIDE + CELLS : PAD_CELLS, :] = zero
    step = 128

    @pl.loop(0, CELLS // step)
    def _(k):
        start = pl.multiple_of(k * step, step)
        near = stage.at[pl.ds(start, step + 16), :]
        rest = []
        for b in (-1, 0, 1):
            off = sign * b
            value = near[8 + off : 8 + off + step, :]
            if off != 0:
                col = lax.broadcasted_iota(jnp.int32, value.shape, 0) % SIDE + off
                value = jnp.where((col >= 0) & (col < SIDE), value, 0.0)
            dst_ref[image, pl.ds(start + SIDE, step), 256 * (b + 1) : 256 * (b + 2)] = (
                value[:, 0:256].astype(BF)
            )
            rest.append(value[:, 256:384])
        low = half_lanes(rest[0].shape)
        first = jnp.where(low, rest[0], pltpu.roll(rest[1], 64, 1))
        second = jnp.where(low, rest[2], 0.0)
        dst_ref[image, pl.ds(start + SIDE, step), 768:896] = first.astype(BF)
        dst_ref[image, pl.ds(start + SIDE, step), 896:1024] = second.astype(BF)


def grad_kernel(x_ref, g_ref, out_ref, stage, cols, flipped, whole):
    for image in range(2):
        flipped[image] = jnp.transpose(x_ref[image])
        build_columns(g_ref, image, stage, cols, -1)
    for row in range(3):
        top = SIDE * (2 - row)
        for part in range(4):
            lanes = pl.ds(256 * part, 256)
            value = jnp.dot(
                flipped[0], cols[0, top : top + CELLS, lanes], preferred_element_type=F32
            ) + jnp.dot(flipped[1], cols[1, top : top + CELLS, lanes], preferred_element_type=F32)
            if part < 3:
                tap = 3 * row + part
                whole[CH * tap : CH * (tap + 1), 0:256] = value
            else:
                pieces = (value[:, 0:128], pltpu.roll(value[:, 0:128], 64, 1), value[:, 128:256])
                for b in range(3):
                    tap = 3 * row + b
                    whole[CH * tap : CH * (tap + 1), 256:384] = pieces[b]

    @pl.loop(0, PARTS // 4)
    def _(q):
        near = whole.at[pl.ds(pl.multiple_of(4 * ROWS * q, 8), 4 * ROWS + 8), :]
        for i in range(4):
            first, second, third = pack_rows(near[ROWS * i : ROWS * i + 96, :])
            j = 4 * q + i
            out_ref[j, 0:96, :] = first.astype(BF)
            out_ref[j, 96:192, :] = second.astype(BF)
            out_ref[j, 192:240, :] = third.astype(BF)


def taps_kernel(w_ref, ahead_ref, back_ref, whole):
    @pl.loop(0, PARTS // 4)
    def _(q):
        near = whole.at[pl.ds(pl.multiple_of(4 * ROWS * q, 8), 4 * ROWS + 8), :]
        for i in range(4):
            base, j = ROWS * i, 4 * q + i
            near[base : base + 96, 0:128] = w_ref[j, 0:96, :].astype(F32)
            near[base : base + 96, 128:256] = w_ref[j, 96:192, :].astype(F32)
            tail = w_ref[j, 192:240, :].astype(F32)
            near[base : base + 48, 256:384] = tail
            near[base + 48 : base + 96, 256:384] = pltpu.roll(tail, 64, 1)

    for row in range(3):
        for b in range(3):
            base = CH * (3 * row + b)
            tap = whole[base : base + CH, :].astype(BF)
            turned = jnp.transpose(tap)
            ahead_ref[row, 256 * b : 256 * (b + 1), :] = tap[0:256]
            ahead_ref[row, 768 + 64 * b : 832 + 64 * b, :] = tap[256:320]
            back_ref[row, 256 * b : 256 * (b + 1), 0:CH] = turned[0:256]
            back_ref[row, 768 + 64 * b : 832 + 64 * b, 0:CH] = turned[256:320]
        ahead_ref[row, 960:1024, :] = jnp.zeros((64, LANES), BF)
        back_ref[row, 960:1024, :] = jnp.zeros((64, LANES), BF)


def conv_kernel(src_ref, taps_ref, *refs, sign):
    out_ref, stage, cols = refs[-3:]
    images = out_ref.shape[0]
    block = 1024
    for image in range(images):
        build_columns(src_ref, image, stage, cols, sign)

        @pl.loop(0, CELLS // block)
        def _(m):
            start = pl.multiple_of(m * block, block)
            value = jnp.zeros((block, LANES), F32)
            for row in range(3):
                top = SIDE * (row if sign > 0 else 2 - row)
                value += jnp.dot(
                    cols[image, pl.ds(start + top, block), :],
                    taps_ref[row],
                    preferred_element_type=F32,
                )
            out_ref[image, pl.ds(start, block), :] = value[:, 0:CH]


def sum_kernel(parts_ref, own_ref, low_ref):
    def body(j, total):
        return total + parts_ref[j].astype(F32)

    own = lax.fori_loop(1, PARTS, body, parts_ref[0].astype(F32))
    own_ref[...] = own
    low_ref[...] = own.astype(BF)


def update_kernel(step_ref, own_ref, other_ref, w_ref, m_ref, far_ref, nw_ref, nm_ref, stage, *, scale):
    both = own_ref[...] + other_ref[...].astype(F32)
    unpack_into(stage, (0.5 * beta_rate) * far_ref[1].astype(F32) + (0.5 * scale) * both)
    rate = peak_rate * (step_ref[0] + 1).astype(F32) / warm_steps
    moment = (0.5 * beta_rate) * m_ref[:, 0, :] + stage[0:ROWS, 0:CH]
    nm_ref[:, 0, :] = moment
    unpack_into(stage, 0.5 * far_ref[0].astype(F32))
    nw_ref[:, 0, :] = 0.5 * w_ref[:, 0, :] + stage[0:ROWS, 0:CH] - rate * moment


def call(kernel, outs, scratch, flops=0, moved=0, **kw):
    return pl.pallas_call(
        kernel,
        out_shape=outs,
        scratch_shapes=scratch,
        compiler_params=pltpu.CompilerParams(vmem_limit_bytes=VMEM_LIMIT),
        cost_estimate=pl.CostEstimate(flops=flops, bytes_accessed=moved, transcendentals=0),
        **kw,
    )


def trade(bit, *values):
    mask = 2**bit
    pairs = [(source, source ^ mask) for source in range(lax.axis_size("group"))]
    return tuple(lax.ppermute(value, "group", pairs) for value in values)


def by_row(value):
    return jnp.transpose(value, (1, 0, 2))


def shards(latents, cotangent, weights, momentum, step):
    images = latents.shape[0]
    bit_count = lax.axis_size("group").bit_length() - 1
    level = step[0] % bit_count
    trades = [partial(trade, bit) for bit in range(bit_count)]
    x = latents.reshape(images, CELLS, CH)
    g = cotangent.reshape(images, CELLS, CH)
    w, m = by_row(weights), by_row(momentum)
    packed = jax.ShapeDtypeStruct((PARTS, PACK, 128), BF)
    stage = pltpu.VMEM((CELLS + 16, LANES), F32)
    cols = pltpu.VMEM((2, PAD_CELLS, COLS), BF)
    whole = pltpu.VMEM((KROWS + 8, LANES), F32)
    conv_flops = 2 * images * CELLS * KROWS * CH
    vmem = pl.BlockSpec(memory_space=pltpu.VMEM)

    piece = jax.ShapeDtypeStruct((PACK, 128), BF)
    pack_stage = pltpu.VMEM((96, LANES), F32)
    spread, w_low = call(spread_kernel, (packed, piece), [pack_stage], moved=2000000)(w)
    m_late, w_low = lax.optimization_barrier((m, w_low))
    pair = call(
        pair_kernel, jax.ShapeDtypeStruct((2, PACK, 128), BF), [pack_stage], moved=300000
    )(w_low, m_late)
    gathered = lax.all_to_all(spread, "shard", 0, 0, tiled=True)

    terms = call(
        grad_kernel, packed,
        [stage, cols, pltpu.VMEM((2, CH, CELLS), BF), whole],
        flops=conv_flops, moved=5000000,
    )(x, g)
    terms, pair = lax.optimization_barrier((terms, pair))
    (far,) = lax.switch(level, trades, pair)
    terms, gathered, far = lax.optimization_barrier((terms, gathered, far))
    received = lax.all_to_all(terms, "shard", 0, 0, tiled=True)
    tap_shape = jax.ShapeDtypeStruct((3, COLS, LANES), BF)
    ahead, behind = call(
        taps_kernel, (tap_shape, tap_shape), [whole], flops=1000000, moved=6000000
    )(gathered)
    out = jax.ShapeDtypeStruct((images, CELLS, CH), F32)
    forward = call(
        partial(conv_kernel, sign=1), out, [stage, cols], flops=conv_flops, moved=6000000
    )(x, ahead)
    backward = call(
        partial(conv_kernel, sign=-1), out, [stage, cols], flops=conv_flops, moved=6000000
    )(g, behind)
    own, own_low = call(
        sum_kernel, (jax.ShapeDtypeStruct((PACK, 128), F32), jax.ShapeDtypeStruct((PACK, 128), BF)),
        [], moved=2000000,
    )(received)
    (other,) = lax.switch(level, trades, own_low)
    cells_group = lax.axis_size("shard") * images * CELLS
    row_shape = jax.ShapeDtypeStruct((ROWS, 1, CH), F32)
    new_w, new_m = call(
        partial(update_kernel, scale=float(cells_group) ** (-0.5)),
        (row_shape, row_shape),
        [pltpu.VMEM((96, LANES), F32)],
        moved=1000000,
        in_specs=[pl.BlockSpec(memory_space=pltpu.SMEM)] + [vmem] * 5,
    )(step, own, other, w, m, far)
    return (
        forward.reshape(latents.shape),
        backward.reshape(latents.shape),
        by_row(new_w),
        by_row(new_m),
    )


def solution(mesh):
    images = P(("group", "shard"), None, None, None)
    rows = P("group", "shard", None)
    return jax.shard_map(
        shards,
        mesh=mesh,
        in_specs=(images, images, rows, rows, P()),
        out_specs=(images, images, rows, rows),
        check_vma=False,
    )
```
